32 devices in a mesh: col: 4 (over y, x), row: 8 (over z, core).
Axes of the slice: x: 2, y: 2, z: 4, core: 2. Of those that a mesh axis runs over, the one named last changes fastest.
Arguments:
- data: bfloat16 [16384, 8192], P('row', 'col'), may hold values from -6 to 6
- column_scale: float32 [8192], P('col'), may hold values from 0.25 to 4
- keep_mask: int32 [16384, 8192], P('row', 'col'), may hold values 0 or 1
Outputs:
- band: float32 [8192, 3, 2048], P('col', None, 'row')
The draws below stay inside these ranges and needn't reach their ends.
All inputs are finite; a program needn't handle non-finite values. No bound on the sum of `keep_mask` on one device may be relied on, other than what follows from the above.
Results may differ from the reference program's by a relative error of at most 0.0012.
Values may be sent and summed in bfloat16 or wider, within the bound.
No kernel may reach another device: no remote copies, remote signals or barrier semaphores. Data moves between devices by JAX's collectives and lax.ppermute only.
A program may use at most 128 MiB of HBM per device.

```python
import math
import jax
import jax.numpy as jnp
from jax import lax

COLS = 8192
ROWS = 16384
PANEL = 2048
HALF = 3
N_COL = 4


def with_ends(values, key, low, top_value):
    shape = values.shape
    index_at = [jax.random.randint(jax.random.fold_in(key, axis), (), 0, shape[axis]) for axis in range(len(shape))]
    values = values.at[tuple(index_at)].set(low)
    longest = shape.index(max(shape))
    index_at[longest] = (index_at[longest] + 1) % shape[longest]
    return values.at[tuple(index_at)].set(top_value)


def levels(key, shape, shards, least, top_value):
    level, own = 1.0, jax.random.fold_in(key, 6)
    for dim, blocks in shards:
        steps = jnp.exp(jax.random.uniform(jax.random.fold_in(own, dim), (blocks,), jnp.float32, least / len(shards), top_value / len(shards)))
        level = level * jnp.repeat(steps, shape[dim] // blocks).reshape([-1 if axis == dim else 1 for axis in range(len(shape))])
    return level


def normal_values(key, dims, deviation, reach, cuts=(), held_as=jnp.bfloat16):
    drawn = jax.random.normal(key, dims, jnp.float32) * deviation
    if len(cuts) > 0:
        drawn = levels(key, dims, cuts, -0.22, 0.18) * drawn
    return jnp.clip(drawn, min=-reach, max=reach).astype(held_as)


def setup_inputs(seed: int = 0) -> dict:
    splits = jax.random.split(jax.random.key(seed), 4)
    data = normal_values(splits[0], (ROWS, COLS), 1.0, 6.0, ((0, 8), (1, 4)))
    column_scale = jnp.clip(jnp.exp(math.log(4.0) - 2.7725887 * jax.random.uniform(splits[1], (COLS,), jnp.float32) ** levels(splits[1], (COLS,), ((0, 4),), -0.2, 0.2)), 0.25, 4.0)
    keep_mask = with_ends((jax.random.randint(splits[2], (ROWS, COLS), 0, 4) < 3).astype(jnp.int32), jax.random.fold_in(splits[2], 1), 0, 1)
    return {"data": data, "column_scale": column_scale, "keep_mask": keep_mask}


def reference(data, column_scale, keep_mask):
    values = data.astype(jnp.float32) * column_scale[None, :]
    colsq = lax.optimization_barrier(jnp.sum(values * values, axis=0))
    divisor = jnp.minimum(jnp.sqrt(colsq + 1.0), jnp.sqrt(jnp.float32(ROWS)))
    scaled = (keep_mask.astype(jnp.float32) * values / divisor[None, :]).astype(jnp.bfloat16)
    wide = scaled.astype(jnp.float32)
    blocks = []
    for panel_index in range(N_COL):
        left = wide[:, panel_index * PANEL:(panel_index + 1) * PANEL]
        rolled = jnp.roll(wide, -panel_index * PANEL, axis=1)[:, :HALF * PANEL]
        tile = jnp.dot(left.T, rolled, precision=lax.Precision.HIGHEST, preferred_element_type=jnp.float32)
        blocks.append(tile.reshape(PANEL, HALF, PANEL))
    return jnp.concatenate(blocks, axis=0)
```

```python
import jax
import jax.numpy as jnp
from jax import lax
from jax.sharding import PartitionSpec as P


def passed_along(block, axis, distance):
    devices = range(lax.axis_size(axis))
    route = [((i - distance) % len(devices), i) for i in devices]
    return lax.ppermute(block, axis, route)


def product(left, right):
    return lax.dot_general(
        left, right, (((0,), (0,)), ((), ())), preferred_element_type=jnp.float32
    )


def reduced(partial, dimension, after):
    if after is not None:
        partial, _ = lax.optimization_barrier((partial, after))
    return lax.psum_scatter(partial, "row", scatter_dimension=dimension, tiled=True)


def mirrored(left, right, offset, after):
    slots = lax.axis_size("row")
    panels = lax.axis_size("col")
    here = lax.axis_index("row")
    width = left.shape[1] // slots
    kept = slots // 2 + 1
    wrapped = jnp.concatenate([left, left[:, : (kept - 1) * width]], axis=1)
    partial = [
        product(wrapped[:, r * width : (r + kept) * width], right[:, r * width : (r + 1) * width])
        for r in range(slots)
    ]
    held = reduced(jnp.concatenate(partial, axis=0), 0, after)
    blocks = [held]
    for d in range(kept, slots):
        e = slots - d
        route = [
            (((c + offset) % panels) * slots + (r + d) % slots, c * slots + r)
            for c in range(panels)
            for r in range(slots)
        ]
        sent = lax.ppermute(held[e * width : (e + 1) * width], ("col", "row"), route)
        blocks.append(sent.T)
    turned = jnp.concatenate(blocks, axis=0)
    twice = jnp.concatenate([turned, turned], axis=0)
    return lax.dynamic_slice_in_dim(twice, (slots - here) * width, slots * width, axis=0), held


def on_device(data, column_scale, keep_mask):
    values = data.astype(jnp.float32) * column_scale[None, :]
    colsq = lax.psum(jnp.sum(values * values, axis=0), "row")
    total_rows = data.shape[0] * lax.axis_size("row")
    divisor = jnp.minimum(jnp.sqrt(colsq + 1.0), jnp.sqrt(jnp.float32(total_rows)))
    scaled = (keep_mask.astype(jnp.float32) * values / divisor[None, :]).astype(jnp.bfloat16)
    offsets = lax.axis_size("col") // 2 + 1
    panels = [scaled]
    current = scaled
    for _ in range(1, offsets):
        current = passed_along(current, "col", -1)
        panels.append(current)
    summed = []
    last = None
    for offset, other in enumerate(panels):
        if (2 * offset) % lax.axis_size("col") == 0:
            block, last = mirrored(scaled, other, offset, last)
        else:
            partial = product(scaled, other)
            block = last = reduced(partial, 1, last)
        summed.append(block)
    return jnp.stack(summed, axis=1)


def solution(mesh):
    in_specs = (P("row", "col"), P("col"), P("row", "col"))
    out_specs = P("col", None, "row")
    return jax.shard_map(
        on_device, mesh=mesh, in_specs=in_specs, out_specs=out_specs, check_vma=False
    )
```
